32 devices in a mesh: row: 8 (over y, x, core), col: 4 (over z).
Axes of the slice: x: 2, y: 2, z: 4, core: 2. Of those that a mesh axis runs over, the one named last changes fastest.
Arguments:
- features: float32 [4096, 128], P(('row', 'col')), may hold values from -6 to 6
- weight: float32 [128, 128], replicated, may hold values from -0.5 to 0.5
- layer_bias: float32 [128], replicated, may hold values from -3 to 3
- degree_scale: float32 [4096], P(('row', 'col')), may hold values from 0.05 to 0.5
- tile_values: bfloat16 [8, 4, 32, 128, 128], P('row', 'col'), may hold values from 0 to 1
- tile_slots: int32 [8, 4, 32], P('row', 'col'), may hold values from 0 to 31, as said below
- tile_count: int32 [8, 4], P('row', 'col'), may hold values from 1 to 32, as said below
- cotangent: float32 [4096, 128], P(('row', 'col')), may hold values from -6 to 6
Outputs:
- activations: float32 [4096, 128], P(('row', 'col'))
- feature_grad: float32 [4096, 128], P(('row', 'col'))
- weight_grad: float32 [128, 128], replicated
- bias_grad: float32 [128], replicated
The draws below stay inside these ranges and needn't reach their ends.
Inputs may be any that keep to these rules, and one draw needn't show every extreme that they name: `tile_slots`: the first tile_count[r, c] slots of a device name distinct positions of its grid of 8 by 4 tiles (row u, column v as p = u * 4 + v); later slots hold other positions in range and are ignored. `tile_count`: counts are skewed across devices; in every draw some device has a full list of 32 tiles.
All inputs are finite; a program needn't handle non-finite values.
Results may differ from the reference program's by a relative error of at most 0.0059.
Values may be sent and summed in bfloat16 or wider, within the bound.
A program may use at most 64 MiB of HBM per device.

```python
import math
import jax
import jax.numpy as jnp
from jax import lax

F = 128
TILE = 128
NBD = 1
MAXT = 32
NODES = 4096
N_ROW = 8
N_COL = 4


def tile_layout(key):
    devices = N_ROW * N_COL
    positions = N_ROW * NBD * N_COL * NBD
    subkeys = jax.random.split(jax.random.fold_in(key, 7), devices)

    def one_device(subkey):
        return jax.random.permutation(subkey, positions)[:MAXT]
    placed = jax.vmap(one_device)(subkeys)
    drawn = jax.random.randint(jax.random.fold_in(key, 11), (devices,), 0, MAXT)
    tile_counts = 1 + drawn * drawn // MAXT
    busiest = jax.random.randint(jax.random.fold_in(key, 13), (), 0, devices)
    tile_counts = jnp.where(jnp.arange(devices) == busiest, MAXT, tile_counts)
    return (placed.reshape(N_ROW, N_COL, MAXT).astype(jnp.int32), tile_counts.reshape(N_ROW, N_COL).astype(jnp.int32))


def draw_tile_slots(key, part):
    placed, tile_counts = tile_layout(key)
    return placed


def draw_tile_count(key, part):
    placed, tile_counts = tile_layout(key)
    return tile_counts


def block_levels(stream_key, shape, cuts, low, largest):
    def one(axis_at, blocks):
        steps = jax.random.uniform(jax.random.fold_in(jax.random.fold_in(stream_key, 6), axis_at), (blocks,), jnp.float32, low / len(cuts), largest / len(cuts))
        return jnp.repeat(jnp.exp(steps), shape[axis_at] // blocks).reshape((-1,) + (1,) * (len(shape) - axis_at - 1))

    level = one(*cuts[0])
    for cut in cuts[1:]:
        level = level * one(*cut)
    return level


def centred(key, shape, deviation, reach, cuts=(), kind=jnp.bfloat16):
    loudness = block_levels(key, shape, cuts, -0.22, 0.18) if cuts else 1.0
    values = jax.random.normal(key, shape, jnp.float32) * deviation * loudness
    return jnp.minimum(jnp.maximum(values, -reach), reach).astype(kind)


def setup_inputs(seed: int = 0) -> dict:
    key_of = jax.random.split(jax.random.key(seed), 9)
    features = centred(key_of[0], (NODES, F), 1.0, 6.0, ((0, 32),), jnp.float32)
    weight = centred(key_of[1], (F, F), F ** -0.5, 0.5, (), jnp.float32)
    layer_bias = centred(key_of[2], (F,), 0.5, 3.0, (), jnp.float32)
    degree_scale = jnp.clip(jnp.exp(math.log(0.5) - 2.3025851 * jax.random.uniform(key_of[3], (NODES,), jnp.float32) ** block_levels(key_of[3], (NODES,), ((0, 32),), -0.2, 0.2)), 0.05, 0.5)
    tile_values = jnp.clip(1.0 * jax.random.uniform(key_of[4], (N_ROW, N_COL, MAXT, TILE, TILE), jnp.float32) ** block_levels(key_of[4], (N_ROW, N_COL, MAXT, TILE, TILE), ((0, 8), (1, 4)), -0.2, 0.2), 0.0, 1.0).astype(jnp.bfloat16)
    tile_slots = draw_tile_slots(jax.random.fold_in(key_of[8], 71), 0)
    tile_count = draw_tile_count(jax.random.fold_in(key_of[8], 71), 0)
    cotangent = centred(key_of[7], (NODES, F), 1.0, 6.0, ((0, 32),), jnp.float32)
    return dict(features=features, weight=weight, layer_bias=layer_bias, degree_scale=degree_scale, tile_values=tile_values, tile_slots=tile_slots, tile_count=tile_count, cotangent=cotangent)


def gelu_pair(values):
    argument = 0.7978845608028654 * (values + 0.044715 * values * values * values)
    tangent = jnp.tanh(argument)
    output = 0.5 * values * (1.0 + tangent)
    slopes = 0.5 * (1.0 + tangent) + 0.5 * values * (1.0 - tangent * tangent) * 0.7978845608028654 * (1.0 + 3.0 * 0.044715 * values * values)
    return (output, slopes)

def reference(features, weight, layer_bias, degree_scale, tile_values, tile_slots, tile_count, cotangent):
    highest = lax.Precision.HIGHEST
    devices = N_ROW * N_COL
    column_blocks = N_COL * NBD
    node_blocks = devices * NBD
    nodes = node_blocks * TILE
    norm_factor = 1.0 / math.sqrt(nodes)
    slots_flat = tile_slots.reshape(devices, MAXT)
    counts_flat = tile_count.reshape(devices)
    values_flat = tile_values.reshape(devices, MAXT, TILE, TILE)

    def placement(device):
        row_index = device // N_COL
        col_index = device % N_COL
        slots = slots_flat[device]
        local_rows = slots // column_blocks
        local_cols = slots % column_blocks
        global_rows = (local_rows // NBD * N_COL + col_index) * NBD + local_rows % NBD
        global_cols = row_index * column_blocks + local_cols
        live_mask = (jnp.arange(MAXT, dtype=jnp.int32) < counts_flat[device]).astype(jnp.float32)
        blocks = values_flat[device].astype(jnp.float32)
        return (global_rows.astype(jnp.int32), global_cols.astype(jnp.int32), live_mask, blocks)
    projected = jnp.dot(features, weight, precision=highest, preferred_element_type=jnp.float32)
    scaled = (degree_scale[:, None] * projected).astype(jnp.bfloat16)
    source_blocks = scaled.astype(jnp.float32).reshape(node_blocks, TILE, F)

    def forward_step(totals, device):
        global_rows, global_cols, live_mask, blocks = placement(device)
        gathered = source_blocks[global_cols]
        products = jnp.einsum('tij,tjf->tif', blocks, gathered, precision=highest) * live_mask[:, None, None]
        return (totals.at[global_rows].add(products), None)
    device_list = jnp.arange(devices, dtype=jnp.int32)
    summed, ignored = lax.scan(forward_step, jnp.zeros((node_blocks, TILE, F), jnp.float32), device_list)
    summed = summed.reshape(nodes, F)
    preact = degree_scale[:, None] * summed + layer_bias[None, :]
    activations, slopes = gelu_pair(preact)
    delta = cotangent * slopes
    bias_grad = lax.optimization_barrier(jnp.sum(delta, axis=0)) * norm_factor
    delta_scaled = (degree_scale[:, None] * delta).astype(jnp.bfloat16)
    delta_blocks = delta_scaled.astype(jnp.float32).reshape(node_blocks, TILE, F)

    def backward_step(totals, device):
        global_rows, global_cols, live_mask, blocks = placement(device)
        gathered = delta_blocks[global_rows]
        products = jnp.einsum('tji,tjf->tif', blocks, gathered, precision=highest) * live_mask[:, None, None]
        return (totals.at[global_cols].add(products), None)
    back_summed, ignored = lax.scan(backward_step, jnp.zeros((node_blocks, TILE, F), jnp.float32), device_list)
    back_summed = back_summed.reshape(nodes, F)
    scaled_grad = degree_scale[:, None] * back_summed
    weight_grad = jnp.dot(features.T, scaled_grad, precision=highest, preferred_element_type=jnp.float32) * norm_factor
    feature_grad = jnp.dot(scaled_grad, weight.T, precision=highest, preferred_element_type=jnp.float32)
    return (activations, feature_grad, weight_grad, bias_grad)
```

```python
import functools
import math

import jax
import jax.numpy as jnp
from jax import lax
from jax.experimental import pallas as pl
from jax.experimental.pallas import tpu as pltpu
from jax.sharding import PartitionSpec as P

MESH = pl.DeviceIdType.MESH
WIRE = jnp.bfloat16


def gelu_pair(values):
    argument = 0.7978845608028654 * (values + 0.044715 * values * values * values)
    tangent = jnp.tanh(argument)
    output = 0.5 * values * (1.0 + tangent)
    slopes = 0.5 * (1.0 + tangent) + 0.5 * values * (
        1.0 - tangent * tangent
    ) * 0.7978845608028654 * (1.0 + 3.0 * 0.044715 * values * values)
    return (output, slopes)


def repeat(count, body):
    if count <= 8:
        for index in range(count):
            body(index)
    else:
        lax.fori_loop(0, count, lambda index, carry: (body(index), carry)[1], 0)


def dot(a, b, **kw):
    return jnp.dot(a, b, preferred_element_type=jnp.float32, **kw)


def halves(values):
    high = values.astype(jnp.bfloat16)
    return high, (values - high.astype(jnp.float32)).astype(jnp.bfloat16)


def stacked_left(matrix):
    high, low = halves(matrix)
    return jnp.concatenate([high, low, high], axis=1)


def stacked_right(values):
    high, low = halves(values)
    return jnp.concatenate([high, high, low], axis=0)


def dot_t(a, b):
    return lax.dot_general(a, b, (((1,), (1,)), ((), ())), preferred_element_type=jnp.float32)


def kernel(
    rows, cols, norm,
    features_hbm, weight_hbm, bias_hbm, degree_hbm, cotangent_hbm, tile_hbm, slot_hbm, count_hbm,
    activation, feature_grad, weight_grad, bias_grad,
    features, weight, bias, degree, cotangent, slot_list, live, found, inverse,
    tiles, dense, dense_t, gathered, part_send, part_recv, delta_all,
    bias_column, cotangent_turned, weight_in, weight_out,
    back_send, back_recv, w_part, w_row, w_col,
    in_sem, tile_sem, found_sem, g_send, g_recv, p_send, p_recv, d_send, d_recv,
    b_send, b_recv, wa_send, wa_recv, wb_send, wb_recv,
):
    own, width = features.shape
    slots, tile, _ = tile_hbm.shape
    sub = own // tile
    places = found.shape[0]
    parts, _, chunk, _ = delta_all.shape
    pairs = rows // 2
    me_r = lax.axis_index("row")
    me_c = lax.axis_index("col")
    me_p, me_k = lax.div(me_r, jnp.int32(2)), lax.rem(me_r, 2)

    def row_peer(step):
        return lax.rem(me_r + step + 1, rows)

    def col_peer(step):
        return lax.rem(me_c + step + 1, cols)

    def pair_at(turn):
        peer, bit = 0, 1
        while bit < pairs:
            flipped = lax.rem(lax.div(me_p, jnp.int32(bit)) + turn // bit, 2)
            peer, bit = peer + bit * flipped, bit * 2
        return peer

    def step_to(peer):
        return lax.rem(peer - me_r - 1 + rows, rows)

    def step_from(peer):
        return lax.rem(me_r - peer - 1 + rows, rows)

    def row_order(turn):
        other = rows - 1 - turn
        peer, bit = 0, 1
        while bit < rows:
            flipped = lax.rem(lax.div(me_r, jnp.int32(bit)) + other // bit, 2)
            peer, bit = peer + bit * flipped, bit * 2
        return step_to(peer)

    def col_order(turn):
        down = cols - 1 - turn
        down = down - lax.div(me_c - down + cols, cols)
        up = turn + lax.div(turn - me_c + cols, cols)
        high = lax.div(me_c * 2, cols)
        peer = high * up + (1 - high) * down
        return lax.rem(peer - me_c - 1 + cols, cols)

    def to_row(step, src, dst, send, recv):
        return pltpu.make_async_remote_copy(
            src_ref=src, dst_ref=dst, send_sem=send.at[step], recv_sem=recv.at[step],
            device_id=(row_peer(step), me_c), device_id_type=MESH,
        )

    def to_col(step, src, dst, send, recv):
        return pltpu.make_async_remote_copy(
            src_ref=src, dst_ref=dst, send_sem=send.at[step], recv_sem=recv.at[step],
            device_id=(me_r, col_peer(step)), device_id_type=MESH,
        )

    barrier = pltpu.get_barrier_semaphore()

    def greet_row(step):
        pl.semaphore_signal(barrier, inc=1, device_id=(row_peer(step), me_c), device_id_type=MESH)

    def greet_col(step):
        pl.semaphore_signal(barrier, inc=1, device_id=(me_r, col_peer(step)), device_id_type=MESH)

    repeat(cols - 1, greet_col)
    repeat(rows - 1, greet_row)
    loads = [
        pltpu.make_async_copy(src, dst, in_sem.at[index])
        for index, (src, dst) in enumerate((
            (features_hbm, features), (degree_hbm, degree), (slot_hbm, slot_list),
            (count_hbm, live), (weight_hbm, weight), (bias_hbm, bias), (cotangent_hbm, cotangent),
        ))
    ]
    for load in loads:
        load.start()
    tile_copy = pltpu.make_async_copy(tile_hbm, tiles.at[pl.ds(0, slots)], tile_sem)
    tile_copy.start()
    tiles[slots] = jnp.zeros((tile, tile), tiles.dtype)
    for load in loads[:4]:
        load.wait()

    scaled = (features[...].T * degree[...]).astype(jnp.bfloat16)
    gathered[me_c] = scaled

    pl.semaphore_wait(barrier, rows + cols - 2)

    def gather_copy(step):
        return to_col(step, gathered.at[me_c], gathered.at[me_c], g_send, g_recv)

    repeat(cols - 1, lambda turn: gather_copy(col_order(turn)).start())

    order = lax.broadcasted_iota(jnp.int32, (places, slots), 1)
    spot = lax.broadcasted_iota(jnp.int32, (places, slots), 0)
    hit = (slot_list[...] == spot) & (order < live[...][:, None])
    nearest = jnp.min(jnp.where(hit, order, slots), axis=1, keepdims=True)
    found[...] = jnp.broadcast_to(nearest, found.shape)
    found_copy = pltpu.make_async_copy(found, inverse, found_sem)
    found_copy.start()
    for load in loads[4:]:
        load.wait()
    turned = weight[...].T
    weight_in[...] = stacked_left(turned)
    for part in range(parts):
        weight_out[part] = stacked_left(weight[:, part * chunk : (part + 1) * chunk])
    bias_column[...] = jnp.broadcast_to(bias[...], (own, width)).T
    cotangent_turned[...] = cotangent[...].T
    found_copy.wait()
    tile_copy.wait()

    def place(pair):
        for u in range(2 * sub):
            for v in range(cols * sub):
                block = tiles[inverse[(pair * 2 * sub + u) * (cols * sub) + v, 0]]
                dense[pair, u * tile : (u + 1) * tile, v * tile : (v + 1) * tile] = block
                dense_t[pair, v * tile : (v + 1) * tile, u * tile : (u + 1) * tile] = block.T

    repeat(pairs, place)

    def part_copy(step):
        return to_row(step, part_send.at[step], part_recv.at[step], p_send, p_recv)

    repeat(cols - 1, lambda step: gather_copy(step).wait_recv())
    source = jnp.concatenate([gathered[v] for v in range(cols)], axis=1)

    def send_pair(turn):
        pair = pair_at(pairs - 1 - turn)
        result = dot(source, dense_t[pair])
        for k in range(2):
            step = step_to(pair * 2 + k)
            part_send[step] = result[:, k * own : (k + 1) * own].astype(WIRE)
            part_copy(step).start()

    repeat(pairs - 1, send_pair)
    result = dot(source, dense_t[me_p])
    first, second = result[:, :own], result[:, own:]
    core = step_to(me_p * 2 + 1 - me_k)
    part_send[core] = jnp.where(me_k == 0, second, first).astype(WIRE)
    part_copy(core).start()
    own_part = jnp.where(me_k == 0, first, second)

    repeat(rows - 1, lambda step: part_copy(step).wait_recv())
    aggregate = own_part + jnp.sum(part_recv[...].astype(jnp.float32), axis=0)
    summed = dot(weight_in[...], stacked_right(aggregate))
    preact = degree[...] * summed + bias_column[...]
    output, slopes = gelu_pair(preact)
    delta = cotangent_turned[...] * slopes
    delta_scaled = (degree[...] * delta).astype(jnp.bfloat16)

    def delta_copy(part, step):
        mine = delta_all.at[part, me_r]
        return to_row(step, mine, mine, d_send.at[part], d_recv.at[part])

    for part in range(parts):
        delta_all[part, me_r] = delta_scaled[part * chunk : (part + 1) * chunk]
        repeat(rows - 1, lambda turn: delta_copy(part, row_order(turn)).start())

    high, low = halves(aggregate)
    w_part[:width] = dot_t(high, delta_scaled) + dot_t(low, delta_scaled)
    w_part[width:] = jnp.broadcast_to(jnp.sum(delta.T, axis=0, keepdims=True), (16, width))
    w_col[me_c] = w_part[...].astype(WIRE)

    def wa_copy(step):
        return to_col(step, w_col.at[me_c], w_col.at[me_c], wa_send, wa_recv)

    repeat(cols - 1, lambda turn: wa_copy(col_order(turn)).start())
    activation[...] = output.T

    def wb_copy(step):
        return to_row(step, w_row.at[me_r], w_row.at[me_r], wb_send, wb_recv)

    def back_copy(part, step):
        return to_col(
            step, back_send.at[part, col_peer(step)], back_recv.at[part, step], b_send.at[part], b_recv.at[part]
        )

    def arrived(part, turn):
        pair = pair_at(turn)
        for k in range(2):
            delta_copy(part, step_from(pair * 2 + k)).wait_recv()

    def back_term(part, pair):
        left = jnp.concatenate([delta_all[part, pair * 2 + k] for k in range(2)], axis=1)
        return dot(left, dense[pair])

    backs = []
    for part in range(parts):
        delta_copy(part, step_from(me_p * 2 + 1 - me_k)).wait_recv()
        total = back_term(part, me_p)

        def add_pair(turn, total):
            arrived(part, turn)
            return total + back_term(part, pair_at(turn))

        if pairs <= 8:
            for turn in range(1, pairs):
                total = add_pair(turn, total)
        else:
            total = lax.fori_loop(1, pairs, add_pair, total)

        mine = jnp.zeros((chunk, own), jnp.float32)
        for v in range(cols):
            block = total[:, v * own : (v + 1) * own]
            mine = jnp.where(me_c == v, block, mine)
            back_send[part, v] = block.astype(WIRE)
        backs.append(mine)
        repeat(cols - 1, lambda turn: back_copy(part, col_order(turn)).start())

    repeat(cols - 1, lambda step: wa_copy(step).wait_recv())
    w_row[me_r] = jnp.sum(w_col[...].astype(jnp.float32), axis=0).astype(WIRE)
    repeat(rows - 1, lambda turn: wb_copy(row_order(turn)).start())

    grad = jnp.zeros((width, own), jnp.float32)
    for part in range(parts):
        repeat(cols - 1, lambda step: back_copy(part, step).wait_recv())
        back_sum = backs[part] + jnp.sum(back_recv[part].astype(jnp.float32), axis=0)
        grad = grad + dot(weight_out[part], stacked_right(degree[...] * back_sum))
    feature_grad[...] = grad.T

    repeat(rows - 1, lambda step: wb_copy(step).wait_recv())
    total = jnp.sum(w_row[...].astype(jnp.float32), axis=0) * norm
    weight_grad[...] = total[:width]
    bias_grad[...] = total[width : width + 1]

    for copy in (gather_copy, wa_copy):
        repeat(cols - 1, lambda step, copy=copy: copy(step).wait_send())
    for copy in (part_copy, wb_copy):
        repeat(rows - 1, lambda step, copy=copy: copy(step).wait_send())
    for part in range(parts):
        repeat(cols - 1, lambda step: back_copy(part, step).wait_send())
        repeat(rows - 1, lambda step: delta_copy(part, step).wait_send())


def write_out(*refs):
    *refs, sem = refs
    half = len(refs) // 2
    copies = [
        pltpu.make_async_copy(refs[index], refs[half + index], sem.at[index])
        for index in range(half)
    ]
    for copy in copies:
        copy.start()
    for copy in copies:
        copy.wait()


def local(
    features, weight, layer_bias, degree_scale, tile_values, tile_slots, tile_count, cotangent
):
    own, width = features.shape
    slots, tile = tile_values.shape[2:4]
    rows = lax.axis_size("row")
    cols = lax.axis_size("col")
    sub = own // tile
    places = rows * sub * cols * sub
    parts = 2
    chunk, pairs = width // parts, rows // 2
    norm = 1.0 / math.sqrt(own * rows * cols)

    f32, bf16, i32 = jnp.float32, jnp.bfloat16, jnp.int32
    vmem = pl.BlockSpec(memory_space=pltpu.VMEM)
    r1, c1 = (rows - 1,), (cols - 1,)
    r2, c2 = (parts, rows - 1), (parts, cols - 1)
    dma = pltpu.SemaphoreType.DMA
    out_shape = (
        jax.ShapeDtypeStruct((own, width), f32),
        jax.ShapeDtypeStruct((own, width), f32),
        jax.ShapeDtypeStruct((width, width), f32),
        jax.ShapeDtypeStruct((1, width), f32),
    )
    outs = pl.pallas_call(
        functools.partial(kernel, rows, cols, norm),
        out_shape=tuple(pltpu.VMEM(out.shape, out.dtype) for out in out_shape),
        in_specs=[pl.BlockSpec(memory_space=pltpu.HBM)] * 8,
        out_specs=(vmem, vmem, vmem, vmem),
        scratch_shapes=[
            pltpu.VMEM((own, width), f32),
            pltpu.VMEM((width, width), f32),
            pltpu.VMEM((1, width), f32),
            pltpu.VMEM((1, own), f32),
            pltpu.VMEM((own, width), f32),
            pltpu.VMEM((1, slots), i32),
            pltpu.VMEM((1,), i32),
            pltpu.VMEM((places, 128), i32),
            pltpu.SMEM((places, 128), i32),
            pltpu.VMEM((slots + 1, tile, tile), bf16),
            pltpu.VMEM((pairs, 2 * own, cols * own), bf16),
            pltpu.VMEM((pairs, cols * own, 2 * own), bf16),
            pltpu.VMEM((cols, width, own), bf16),
            pltpu.VMEM((rows - 1, width, own), WIRE),
            pltpu.VMEM((rows - 1, width, own), WIRE),
            pltpu.VMEM((parts, rows, chunk, own), bf16),
            pltpu.VMEM((width, own), f32),
            pltpu.VMEM((width, own), f32),
            pltpu.VMEM((width, 3 * width), bf16),
            pltpu.VMEM((parts, width, 3 * chunk), bf16),
            pltpu.VMEM((parts, cols, chunk, own), WIRE),
            pltpu.VMEM((parts, cols - 1, chunk, own), WIRE),
            pltpu.VMEM((width + 16, width), f32),
            pltpu.VMEM((rows, width + 16, width), WIRE),
            pltpu.VMEM((cols, width + 16, width), WIRE),
            dma((7,)), dma, dma, dma(c1), dma(c1), dma(r1), dma(r1), dma(r2), dma(r2),
            dma(c2), dma(c2), dma(c1), dma(c1), dma(r1), dma(r1),
        ],
        compiler_params=pltpu.CompilerParams(collective_id=0, has_side_effects=True),
        name="graph_layer",
    )(
        features, weight, layer_bias.reshape(1, width), degree_scale.reshape(1, own),
        cotangent, tile_values.reshape(slots, tile, tile), tile_slots.reshape(1, slots),
        tile_count.reshape(1),
    )
    outs = pl.pallas_call(
        write_out,
        out_shape=out_shape,
        in_specs=[vmem] * 4,
        out_specs=[pl.BlockSpec(memory_space=pltpu.HBM)] * 4,
        scratch_shapes=[dma((4,))],
        name="write_out",
    )(*[pltpu.with_memory_space_constraint(out, pltpu.VMEM) for out in outs])
    return (outs[0], outs[1], outs[2], outs[3].reshape(width))


def solution(mesh):
    return jax.shard_map(
        local,
        mesh=mesh,
        in_specs=(
            P(("row", "col"), None),
            P(),
            P(),
            P(("row", "col")),
            P("row", "col", None, None, None),
            P("row", "col", None),
            P("row", "col"),
            P(("row", "col"), None),
        ),
        out_specs=(P(("row", "col"), None), P(("row", "col"), None), P(), P()),
        check_vma=False,
    )
```

```python
import functools
import math

import jax
import jax.numpy as jnp
from jax import lax
from jax.experimental import pallas as pl
from jax.experimental.pallas import tpu as pltpu
from jax.sharding import PartitionSpec as P

MESH = pl.DeviceIdType.MESH
WIRE = jnp.bfloat16


def gelu_pair(values):
    argument = 0.7978845608028654 * (values + 0.044715 * values * values * values)
    tangent = jnp.tanh(argument)
    output = 0.5 * values * (1.0 + tangent)
    slopes = 0.5 * (1.0 + tangent) + 0.5 * values * (
        1.0 - tangent * tangent
    ) * 0.7978845608028654 * (1.0 + 3.0 * 0.044715 * values * values)
    return (output, slopes)


def repeat(count, body):
    if count <= 8:
        for index in range(count):
            body(index)
    else:
        lax.fori_loop(0, count, lambda index, carry: (body(index), carry)[1], 0)


def dot(a, b, **kw):
    return jnp.dot(a, b, preferred_element_type=jnp.float32, **kw)


def halves(values):
    high = values.astype(jnp.bfloat16)
    return high, (values - high.astype(jnp.float32)).astype(jnp.bfloat16)


def stacked_left(matrix):
    high, low = halves(matrix)
    return jnp.concatenate([high, low, high], axis=1)


def stacked_right(values):
    high, low = halves(values)
    return jnp.concatenate([high, high, low], axis=0)


def dot_t(a, b):
    return lax.dot_general(a, b, (((1,), (1,)), ((), ())), preferred_element_type=jnp.float32)


def kernel(
    rows, cols, norm,
    features_hbm, weight_hbm, bias_hbm, degree_hbm, cotangent_hbm, tile_hbm, slot_hbm, count_hbm,
    activation, feature_grad, weight_grad, bias_grad,
    features, weight, bias, degree, cotangent, slot_list, live, found, inverse,
    tiles, dense, dense_t, gathered, part_send, part_recv, delta_all,
    bias_column, cotangent_turned, weight_in, weight_out,
    back_send, back_recv, w_part, w_core, w_col, w_row,
    in_sem, tile_sem, found_sem, g_send, g_recv, p_send, p_recv, d_send, d_recv,
    b_send, b_recv, wa_send, wa_recv, wb_send, wb_recv, wc_send, wc_recv,
):
    own, width = features.shape
    slots, tile, _ = tile_hbm.shape
    sub = own // tile
    places = found.shape[0]
    parts, _, chunk, _ = delta_all.shape
    pairs, half = rows // 2, width // 2
    me_r = lax.axis_index("row")
    me_c = lax.axis_index("col")
    me_p, me_k = lax.div(me_r, jnp.int32(2)), lax.rem(me_r, 2)

    def row_peer(step):
        return lax.rem(me_r + step + 1, rows)

    def col_peer(step):
        return lax.rem(me_c + step + 1, cols)

    def pair_at(turn):
        peer, bit = 0, 1
        while bit < pairs:
            flipped = lax.rem(lax.div(me_p, jnp.int32(bit)) + turn // bit, 2)
            peer, bit = peer + bit * flipped, bit * 2
        return peer

    def step_to(peer):
        return lax.rem(peer - me_r - 1 + rows, rows)

    def step_from(peer):
        return lax.rem(me_r - peer - 1 + rows, rows)

    def row_order(turn):
        other = rows - 1 - turn
        peer, bit = 0, 1
        while bit < rows:
            flipped = lax.rem(lax.div(me_r, jnp.int32(bit)) + other // bit, 2)
            peer, bit = peer + bit * flipped, bit * 2
        return step_to(peer)

    def col_order(turn):
        down = cols - 1 - turn
        down = down - lax.div(me_c - down + cols, cols)
        up = turn + lax.div(turn - me_c + cols, cols)
        high = lax.div(me_c * 2, cols)
        peer = high * up + (1 - high) * down
        return lax.rem(peer - me_c - 1 + cols, cols)

    def row_first(turn):
        return step_to(turn + lax.div(turn - me_r + rows, rows))

    def col_first(turn):
        peer = turn + lax.div(turn - me_c + cols, cols)
        return lax.rem(peer - me_c - 1 + cols, cols)

    def to_row(step, src, dst, send, recv):
        return pltpu.make_async_remote_copy(
            src_ref=src, dst_ref=dst, send_sem=send.at[step], recv_sem=recv.at[step],
            device_id=(row_peer(step), me_c), device_id_type=MESH,
        )

    def to_col(step, src, dst, send, recv):
        return pltpu.make_async_remote_copy(
            src_ref=src, dst_ref=dst, send_sem=send.at[step], recv_sem=recv.at[step],
            device_id=(me_r, col_peer(step)), device_id_type=MESH,
        )

    barrier = pltpu.get_barrier_semaphore()

    def greet_row(step):
        pl.semaphore_signal(barrier, inc=1, device_id=(row_peer(step), me_c), device_id_type=MESH)

    def greet_col(step):
        pl.semaphore_signal(barrier, inc=1, device_id=(me_r, col_peer(step)), device_id_type=MESH)

    repeat(cols - 1, greet_col)
    repeat(rows - 1, greet_row)
    loads = [
        pltpu.make_async_copy(src, dst, in_sem.at[index])
        for index, (src, dst) in enumerate((
            (features_hbm, features), (degree_hbm, degree), (slot_hbm, slot_list),
            (count_hbm, live), (weight_hbm, weight), (bias_hbm, bias), (cotangent_hbm, cotangent),
        ))
    ]
    for load in loads:
        load.start()
    tile_copy = pltpu.make_async_copy(tile_hbm, tiles.at[pl.ds(0, slots)], tile_sem)
    tile_copy.start()
    tiles[slots] = jnp.zeros((tile, tile), tiles.dtype)
    for load in loads[:4]:
        load.wait()

    scaled = (features[...].T * degree[...]).astype(jnp.bfloat16)
    gathered[me_c] = scaled

    pl.semaphore_wait(barrier, rows + cols - 2)

    def gather_copy(step):
        return to_col(step, gathered.at[me_c], gathered.at[me_c], g_send, g_recv)

    repeat(cols - 1, lambda turn: gather_copy(col_order(turn)).start())

    order = lax.broadcasted_iota(jnp.int32, (places, slots), 1)
    spot = lax.broadcasted_iota(jnp.int32, (places, slots), 0)
    hit = (slot_list[...] == spot) & (order < live[...][:, None])
    nearest = jnp.min(jnp.where(hit, order, slots), axis=1, keepdims=True)
    found[...] = jnp.broadcast_to(nearest, found.shape)
    found_copy = pltpu.make_async_copy(found, inverse, found_sem)
    found_copy.start()
    for load in loads[4:]:
        load.wait()
    turned = weight[...].T
    weight_in[...] = stacked_left(turned)
    for part in range(parts):
        weight_out[part] = stacked_left(weight[:, part * chunk : (part + 1) * chunk])
    bias_column[...] = jnp.broadcast_to(bias[...], (own, width)).T
    cotangent_turned[...] = cotangent[...].T
    found_copy.wait()
    tile_copy.wait()

    def place(pair):
        for u in range(2 * sub):
            for v in range(cols * sub):
                block = tiles[inverse[(pair * 2 * sub + u) * (cols * sub) + v, 0]]
                dense[pair, u * tile : (u + 1) * tile, v * tile : (v + 1) * tile] = block
                dense_t[pair, v * tile : (v + 1) * tile, u * tile : (u + 1) * tile] = block.T

    repeat(pairs, place)

    def part_copy(step):
        return to_row(step, part_send.at[step], part_recv.at[step], p_send, p_recv)

    repeat(cols - 1, lambda step: gather_copy(step).wait_recv())
    source = jnp.concatenate([gathered[v] for v in range(cols)], axis=1)

    def send_pair(turn):
        pair = pair_at(pairs - 1 - turn)
        result = dot(source, dense_t[pair])
        for k in range(2):
            step = step_to(pair * 2 + k)
            part_send[step] = result[:, k * own : (k + 1) * own].astype(WIRE)
            part_copy(step).start()

    repeat(pairs - 1, send_pair)
    result = dot(source, dense_t[me_p])
    first, second = result[:, :own], result[:, own:]
    core = step_to(me_p * 2 + 1 - me_k)
    part_send[core] = jnp.where(me_k == 0, second, first).astype(WIRE)
    part_copy(core).start()
    own_part = jnp.where(me_k == 0, first, second)

    repeat(rows - 1, lambda step: part_copy(step).wait_recv())
    aggregate = own_part + jnp.sum(part_recv[...].astype(jnp.float32), axis=0)
    stacked = stacked_right(aggregate)

    def delta_copy(part, step):
        mine = delta_all.at[part, me_r]
        return to_row(step, mine, mine, d_send.at[part], d_recv.at[part])

    outputs, deltas = [], []
    for part in range(parts):
        span = slice(part * chunk, (part + 1) * chunk)
        summed = dot(weight_in[span], stacked)
        output, slopes = gelu_pair(degree[...] * summed + bias_column[span])
        delta = cotangent_turned[span] * slopes
        delta_all[part, me_r] = (degree[...] * delta).astype(jnp.bfloat16)
        repeat(rows - 1, lambda turn: delta_copy(part, row_first(turn)).start())
        outputs.append(output)
        deltas.append(delta)
    output, delta = jnp.concatenate(outputs, axis=0), jnp.concatenate(deltas, axis=0)
    delta_scaled = jnp.concatenate([delta_all[part, me_r] for part in range(parts)], axis=0)

    high, low = halves(aggregate)
    terms = dot_t(high, delta_scaled) + dot_t(low, delta_scaled)
    bias_term = jnp.broadcast_to(jnp.sum(delta.T, axis=0, keepdims=True), (8, width))
    for k in range(2):
        w_part[k, :half] = terms[k * half : (k + 1) * half]
        w_part[k, half:] = bias_term

    def to_core(src, dst, send, recv):
        return pltpu.make_async_remote_copy(
            src_ref=src, dst_ref=dst, send_sem=send, recv_sem=recv,
            device_id=(me_p * 2 + 1 - me_k, me_c), device_id_type=MESH,
        )

    split_copy = to_core(w_part.at[1 - me_k], w_core, wc_send, wc_recv)
    split_copy.start()
    activation[...] = output.T
    split_copy.wait_recv()

    def packed(values):
        values = values.astype(WIRE)
        return values[:half], jnp.broadcast_to(values[half : half + 1], (16, width))

    w_col[me_c, :half], w_col[me_c, half:] = packed(w_part[me_k] + w_core[...])

    def wa_copy(step):
        return to_col(step, w_col.at[me_c], w_col.at[me_c], wa_send, wa_recv)

    repeat(cols - 1, lambda turn: wa_copy(col_order(turn)).start())

    def wb_copy(step):
        return to_row(step, w_row.at[me_r], w_row.at[me_r], wb_send, wb_recv)

    def back_copy(part, step):
        return to_col(
            step, back_send.at[part, col_peer(step)], back_recv.at[part, step], b_send.at[part], b_recv.at[part]
        )

    def arrived(part, turn):
        pair = pair_at(turn)
        for k in range(2):
            delta_copy(part, step_from(pair * 2 + k)).wait_recv()

    def back_term(part, pair):
        left = jnp.concatenate([delta_all[part, pair * 2 + k] for k in range(2)], axis=1)
        return dot(left, dense[pair])

    backs = []
    for part in range(parts):
        delta_copy(part, step_from(me_p * 2 + 1 - me_k)).wait_recv()
        total = back_term(part, me_p)

        def add_pair(turn, total):
            arrived(part, turn)
            return total + back_term(part, pair_at(turn))

        if pairs <= 8:
            for turn in range(1, pairs):
                total = add_pair(turn, total)
        else:
            total = lax.fori_loop(1, pairs, add_pair, total)

        mine = jnp.zeros((chunk, own), jnp.float32)
        for v in range(cols):
            block = total[:, v * own : (v + 1) * own]
            mine = jnp.where(me_c == v, block, mine)
            back_send[part, v] = block.astype(WIRE)
        backs.append(mine)
        back_copy(part, col_first(0)).start()

    repeat(cols - 1, lambda step: wa_copy(step).wait_recv())
    w_row[me_r] = jnp.sum(w_col[...].astype(jnp.float32), axis=0).astype(WIRE)
    repeat(rows - 1, lambda turn: wb_copy(row_order(turn)).start())
    for part in range(parts):
        repeat(cols - 2, lambda turn: back_copy(part, col_first(turn + 1)).start())


    grad = jnp.zeros((width, own), jnp.float32)
    for part in range(parts):
        if part == parts - 1:
            repeat(rows - 1, lambda step: wb_copy(step).wait_recv())
            for k in range(2):
                total = w_row[k].astype(jnp.float32)
                for pair in range(1, pairs):
                    total = total + w_row[2 * pair + k].astype(jnp.float32)
                weight_grad[k * half : (k + 1) * half] = total[:half] * norm
                if k == 0:
                    bias_grad[...] = total[half : half + 1] * norm

        repeat(cols - 1, lambda step: back_copy(part, step).wait_recv())
        back_sum = backs[part] + jnp.sum(back_recv[part].astype(jnp.float32), axis=0)
        grad = grad + dot(weight_out[part], stacked_right(degree[...] * back_sum))
    feature_grad[...] = grad.T

    split_copy.wait_send()
    repeat(rows - 1, lambda step: wb_copy(step).wait_send())
    for copy in (gather_copy, wa_copy):
        repeat(cols - 1, lambda step, copy=copy: copy(step).wait_send())
    repeat(rows - 1, lambda step: part_copy(step).wait_send())
    for part in range(parts):
        repeat(cols - 1, lambda step: back_copy(part, step).wait_send())
        repeat(rows - 1, lambda step: delta_copy(part, step).wait_send())


def write_out(*refs):
    *refs, sem = refs
    half = len(refs) // 2
    copies = [
        pltpu.make_async_copy(refs[index], refs[half + index], sem.at[index])
        for index in range(half)
    ]
    for copy in copies:
        copy.start()
    for copy in copies:
        copy.wait()


def local(
    features, weight, layer_bias, degree_scale, tile_values, tile_slots, tile_count, cotangent
):
    own, width = features.shape
    slots, tile = tile_values.shape[2:4]
    rows = lax.axis_size("row")
    cols = lax.axis_size("col")
    sub = own // tile
    places = rows * sub * cols * sub
    parts = 2
    chunk, half, pairs = width // parts, width // 2, rows // 2
    norm = 1.0 / math.sqrt(own * rows * cols)

    f32, bf16, i32 = jnp.float32, jnp.bfloat16, jnp.int32
    vmem = pl.BlockSpec(memory_space=pltpu.VMEM)
    r1, c1 = (rows - 1,), (cols - 1,)
    r2, c2 = (parts, rows - 1), (parts, cols - 1)
    dma = pltpu.SemaphoreType.DMA
    out_shape = (
        jax.ShapeDtypeStruct((own, width), f32),
        jax.ShapeDtypeStruct((own, width), f32),
        jax.ShapeDtypeStruct((width, width), f32),
        jax.ShapeDtypeStruct((1, width), f32),
    )
    outs = pl.pallas_call(
        functools.partial(kernel, rows, cols, norm),
        out_shape=tuple(pltpu.VMEM(out.shape, out.dtype) for out in out_shape),
        in_specs=[pl.BlockSpec(memory_space=pltpu.HBM)] * 8,
        out_specs=(vmem, vmem, vmem, vmem),
        scratch_shapes=[
            pltpu.VMEM((own, width), f32),
            pltpu.VMEM((width, width), f32),
            pltpu.VMEM((1, width), f32),
            pltpu.VMEM((1, own), f32),
            pltpu.VMEM((own, width), f32),
            pltpu.VMEM((1, slots), i32),
            pltpu.VMEM((1,), i32),
            pltpu.VMEM((places, 128), i32),
            pltpu.SMEM((places, 128), i32),
            pltpu.VMEM((slots + 1, tile, tile), bf16),
            pltpu.VMEM((pairs, 2 * own, cols * own), bf16),
            pltpu.VMEM((pairs, cols * own, 2 * own), bf16),
            pltpu.VMEM((cols, width, own), bf16),
            pltpu.VMEM((rows - 1, width, own), WIRE),
            pltpu.VMEM((rows - 1, width, own), WIRE),
            pltpu.VMEM((parts, rows, chunk, own), bf16),
            pltpu.VMEM((width, own), f32),
            pltpu.VMEM((width, own), f32),
            pltpu.VMEM((width, 3 * width), bf16),
            pltpu.VMEM((parts, width, 3 * chunk), bf16),
            pltpu.VMEM((parts, cols, chunk, own), WIRE),
            pltpu.VMEM((parts, cols - 1, chunk, own), WIRE),
            pltpu.VMEM((2, half + 8, width), f32),
            pltpu.VMEM((half + 8, width), f32),
            pltpu.VMEM((cols, half + 16, width), WIRE),
            pltpu.VMEM((rows, half + 16, width), WIRE),
            dma((7,)), dma, dma, dma(c1), dma(c1), dma(r1), dma(r1), dma(r2), dma(r2),
            dma(c2), dma(c2), dma(c1), dma(c1), dma(r1), dma(r1), dma, dma,
        ],
        compiler_params=pltpu.CompilerParams(collective_id=0, has_side_effects=True),
        name="graph_layer",
    )(
        features, weight, layer_bias.reshape(1, width), degree_scale.reshape(1, own),
        cotangent, tile_values.reshape(slots, tile, tile), tile_slots.reshape(1, slots),
        tile_count.reshape(1),
    )
    outs = pl.pallas_call(
        write_out,
        out_shape=out_shape,
        in_specs=[vmem] * 4,
        out_specs=[pl.BlockSpec(memory_space=pltpu.HBM)] * 4,
        scratch_shapes=[dma((4,))],
        name="write_out",
    )(*[pltpu.with_memory_space_constraint(out, pltpu.VMEM) for out in outs])
    return (outs[0], outs[1], outs[2], outs[3].reshape(width))


def solution(mesh):
    return jax.shard_map(
        local,
        mesh=mesh,
        in_specs=(
            P(("row", "col"), None),
            P(),
            P(),
            P(("row", "col")),
            P("row", "col", None, None, None),
            P("row", "col", None),
            P("row", "col"),
            P(("row", "col"), None),
        ),
        out_specs=(P(("row", "col"), None), P(("row", "col"), None), P(), P()),
        check_vma=False,
    )
```

```python
import functools
import math

import jax
import jax.numpy as jnp
from jax import lax
from jax.experimental import pallas as pl
from jax.experimental.pallas import tpu as pltpu
from jax.sharding import PartitionSpec as P

MESH = pl.DeviceIdType.MESH
WIRE = jnp.bfloat16


def gelu_pair(values):
    argument = 0.7978845608028654 * (values + 0.044715 * values * values * values)
    tangent = jnp.tanh(argument)
    output = 0.5 * values * (1.0 + tangent)
    slopes = 0.5 * (1.0 + tangent) + 0.5 * values * (
        1.0 - tangent * tangent
    ) * 0.7978845608028654 * (1.0 + 3.0 * 0.044715 * values * values)
    return (output, slopes)


def repeat(count, body):
    if count <= 8:
        for index in range(count):
            body(index)
    else:
        lax.fori_loop(0, count, lambda index, carry: (body(index), carry)[1], 0)


def dot(a, b, **kw):
    return jnp.dot(a, b, preferred_element_type=jnp.float32, **kw)


def halves(values):
    high = values.astype(jnp.bfloat16)
    return high, (values - high.astype(jnp.float32)).astype(jnp.bfloat16)


def stacked_left(matrix):
    high, low = halves(matrix)
    return jnp.concatenate([high, low, high], axis=1)


def stacked_right(values):
    high, low = halves(values)
    return jnp.concatenate([high, high, low], axis=0)


def dot_t(a, b):
    return lax.dot_general(a, b, (((1,), (1,)), ((), ())), preferred_element_type=jnp.float32)


def kernel(
    rows, cols, norm,
    features_hbm, weight_hbm, bias_hbm, degree_hbm, cotangent_hbm, tile_hbm, slot_hbm, count_hbm,
    activation, feature_grad, weight_grad, bias_grad,
    features, weight, bias, degree, cotangent, slot_list, live, found, inverse,
    tiles, dense, dense_t, gathered, part_send, part_recv, delta_all,
    bias_column, cotangent_turned, weight_in, weight_out,
    back_send, back_recv, w_part, w_core, w_col, w_row,
    in_sem, tile_sem, found_sem, g_send, g_recv, p_send, p_recv, d_send, d_recv,
    b_send, b_recv, wa_send, wa_recv, wb_send, wb_recv, wc_send, wc_recv,
):
    own, width = features.shape
    slots, tile, _ = tile_hbm.shape
    sub = own // tile
    places = found.shape[0]
    parts, _, chunk, _ = delta_all.shape
    pairs, half = rows // 2, width // 2
    me_r = lax.axis_index("row")
    me_c = lax.axis_index("col")
    me_p, me_k = lax.div(me_r, jnp.int32(2)), lax.rem(me_r, 2)

    def row_peer(step):
        return lax.rem(me_r + step + 1, rows)

    def col_peer(step):
        return lax.rem(me_c + step + 1, cols)

    def pair_at(turn):
        peer, bit = 0, 1
        while bit < pairs:
            flipped = lax.rem(lax.div(me_p, jnp.int32(bit)) + turn // bit, 2)
            peer, bit = peer + bit * flipped, bit * 2
        return peer

    def step_to(peer):
        return lax.rem(peer - me_r - 1 + rows, rows)

    def step_from(peer):
        return lax.rem(me_r - peer - 1 + rows, rows)

    def row_order(turn):
        other = rows - 1 - turn
        peer, bit = 0, 1
        while bit < rows:
            flipped = lax.rem(lax.div(me_r, jnp.int32(bit)) + other // bit, 2)
            peer, bit = peer + bit * flipped, bit * 2
        return step_to(peer)

    def col_order(turn):
        down = cols - 1 - turn
        down = down - lax.div(me_c - down + cols, cols)
        up = turn + lax.div(turn - me_c + cols, cols)
        high = lax.div(me_c * 2, cols)
        peer = high * up + (1 - high) * down
        return lax.rem(peer - me_c - 1 + cols, cols)

    def row_first(turn):
        return step_to(turn + lax.div(turn - me_r + rows, rows))

    def col_first(turn):
        peer = turn + lax.div(turn - me_c + cols, cols)
        return lax.rem(peer - me_c - 1 + cols, cols)

    def to_row(step, src, dst, send, recv):
        return pltpu.make_async_remote_copy(
            src_ref=src, dst_ref=dst, send_sem=send.at[step], recv_sem=recv.at[step],
            device_id=(row_peer(step), me_c), device_id_type=MESH,
        )

    def to_col(step, src, dst, send, recv):
        return pltpu.make_async_remote_copy(
            src_ref=src, dst_ref=dst, send_sem=send.at[step], recv_sem=recv.at[step],
            device_id=(me_r, col_peer(step)), device_id_type=MESH,
        )

    barrier = pltpu.get_barrier_semaphore()

    def greet_row(step):
        pl.semaphore_signal(barrier, inc=1, device_id=(row_peer(step), me_c), device_id_type=MESH)

    def greet_col(step):
        pl.semaphore_signal(barrier, inc=1, device_id=(me_r, col_peer(step)), device_id_type=MESH)

    repeat(cols - 1, greet_col)
    repeat(rows - 1, greet_row)
    loads = [
        pltpu.make_async_copy(src, dst, in_sem.at[index])
        for index, (src, dst) in enumerate((
            (features_hbm, features), (degree_hbm, degree), (slot_hbm, slot_list),
            (count_hbm, live), (weight_hbm, weight), (bias_hbm, bias), (cotangent_hbm, cotangent),
        ))
    ]
    for load in loads:
        load.start()
    tile_copy = pltpu.make_async_copy(tile_hbm, tiles.at[pl.ds(0, slots)], tile_sem)
    tile_copy.start()
    for load in loads[:2]:
        load.wait()

    scaled = (features[...].T * degree[...]).astype(jnp.bfloat16)
    gathered[me_c] = scaled

    pl.semaphore_wait(barrier, rows + cols - 2)

    def gather_copy(step):
        return to_col(step, gathered.at[me_c], gathered.at[me_c], g_send, g_recv)

    repeat(cols - 1, lambda turn: gather_copy(col_order(turn)).start())

    tiles[slots] = jnp.zeros((tile, tile), tiles.dtype)
    for load in loads[2:4]:
        load.wait()
    order = lax.broadcasted_iota(jnp.int32, (places, slots), 1)
    spot = lax.broadcasted_iota(jnp.int32, (places, slots), 0)
    hit = (slot_list[...] == spot) & (order < live[...][:, None])
    nearest = jnp.min(jnp.where(hit, order, slots), axis=1, keepdims=True)
    found[...] = jnp.broadcast_to(nearest, found.shape)
    found_copy = pltpu.make_async_copy(found, inverse, found_sem)
    found_copy.start()
    for load in loads[4:]:
        load.wait()
    turned = weight[...].T
    weight_in[...] = stacked_left(turned)
    for part in range(parts):
        weight_out[part] = stacked_left(weight[:, part * chunk : (part + 1) * chunk])
    bias_column[...] = jnp.broadcast_to(bias[...], (own, width)).T
    cotangent_turned[...] = cotangent[...].T
    found_copy.wait()
    tile_copy.wait()

    def place(pair):
        for u in range(2 * sub):
            for v in range(cols * sub):
                block = tiles[inverse[(pair * 2 * sub + u) * (cols * sub) + v, 0]]
                dense[pair, u * tile : (u + 1) * tile, v * tile : (v + 1) * tile] = block
                dense_t[pair, v * tile : (v + 1) * tile, u * tile : (u + 1) * tile] = block.T

    repeat(pairs, place)

    def part_copy(step):
        return to_row(step, part_send.at[step], part_recv.at[step], p_send, p_recv)

    repeat(cols - 1, lambda step: gather_copy(step).wait_recv())
    source = jnp.concatenate([gathered[v] for v in range(cols)], axis=1)

    def send_pair(turn):
        pair = pair_at(pairs - 1 - turn)
        result = dot(source, dense_t[pair])
        for k in range(2):
            step = step_to(pair * 2 + k)
            part_send[step] = result[:, k * own : (k + 1) * own].astype(WIRE)
            part_copy(step).start()

    repeat(pairs - 1, send_pair)
    result = dot(source, dense_t[me_p])
    first, second = result[:, :own], result[:, own:]
    core = step_to(me_p * 2 + 1 - me_k)
    part_send[core] = jnp.where(me_k == 0, second, first).astype(WIRE)
    part_copy(core).start()
    own_part = jnp.where(me_k == 0, first, second)

    def add_part(peer, total):
        step = step_from(peer)
        part_copy(step).wait_recv()
        return total + part_recv[step].astype(jnp.float32)

    def add_parts(turn, total):
        pair = pair_at(turn)
        return add_part(pair * 2 + 1, add_part(pair * 2, total))

    aggregate = add_part(me_p * 2 + 1 - me_k, own_part)
    if pairs <= 8:
        for turn in range(1, pairs):
            aggregate = add_parts(turn, aggregate)
    else:
        aggregate = lax.fori_loop(1, pairs, add_parts, aggregate)
    stacked = stacked_right(aggregate)

    def delta_copy(part, step):
        mine = delta_all.at[part, me_r]
        return to_row(step, mine, mine, d_send.at[part], d_recv.at[part])

    outputs, deltas = [], []
    for part in range(parts):
        span = slice(part * chunk, (part + 1) * chunk)
        summed = dot(weight_in[span], stacked)
        output, slopes = gelu_pair(degree[...] * summed + bias_column[span])
        delta = cotangent_turned[span] * slopes
        delta_all[part, me_r] = (degree[...] * delta).astype(jnp.bfloat16)
        repeat(rows - 1, lambda turn: delta_copy(part, row_first(turn)).start())
        outputs.append(output)
        deltas.append(delta)
    output, delta = jnp.concatenate(outputs, axis=0), jnp.concatenate(deltas, axis=0)
    delta_scaled = jnp.concatenate([delta_all[part, me_r] for part in range(parts)], axis=0)

    high, low = halves(aggregate)
    terms = dot_t(high, delta_scaled) + dot_t(low, delta_scaled)
    bias_term = jnp.broadcast_to(jnp.sum(delta.T, axis=0, keepdims=True), (8, width))
    for k in range(2):
        w_part[k, :half] = terms[k * half : (k + 1) * half]
        w_part[k, half:] = bias_term

    def to_core(src, dst, send, recv):
        return pltpu.make_async_remote_copy(
            src_ref=src, dst_ref=dst, send_sem=send, recv_sem=recv,
            device_id=(me_p * 2 + 1 - me_k, me_c), device_id_type=MESH,
        )

    split_copy = to_core(w_part.at[1 - me_k], w_core, wc_send, wc_recv)
    split_copy.start()
    activation[...] = output.T
    split_copy.wait_recv()

    def packed(values):
        values = values.astype(WIRE)
        return values[:half], jnp.broadcast_to(values[half : half + 1], (16, width))

    w_col[me_c, :half], w_col[me_c, half:] = packed(w_part[me_k] + w_core[...])

    def wa_copy(step):
        return to_col(step, w_col.at[me_c], w_col.at[me_c], wa_send, wa_recv)

    repeat(cols - 1, lambda turn: wa_copy(col_order(turn)).start())

    def wb_copy(step):
        return to_row(step, w_row.at[me_r], w_row.at[me_r], wb_send, wb_recv)

    def back_copy(part, step):
        return to_col(
            step, back_send.at[part, col_peer(step)], back_recv.at[part, step], b_send.at[part], b_recv.at[part]
        )

    def arrived(part, turn):
        pair = pair_at(turn)
        for k in range(2):
            delta_copy(part, step_from(pair * 2 + k)).wait_recv()

    def back_term(part, pair):
        left = jnp.concatenate([delta_all[part, pair * 2 + k] for k in range(2)], axis=1)
        return dot(left, dense[pair])

    backs = []
    for part in range(parts):
        delta_copy(part, step_from(me_p * 2 + 1 - me_k)).wait_recv()
        total = back_term(part, me_p)

        def add_pair(turn, total):
            arrived(part, turn)
            return total + back_term(part, pair_at(turn))

        if pairs <= 8:
            for turn in range(1, pairs):
                total = add_pair(turn, total)
        else:
            total = lax.fori_loop(1, pairs, add_pair, total)

        mine = jnp.zeros((chunk, own), jnp.float32)
        for v in range(cols):
            block = total[:, v * own : (v + 1) * own]
            mine = jnp.where(me_c == v, block, mine)
            back_send[part, v] = block.astype(WIRE)
        backs.append(mine)
        back_copy(part, col_first(0)).start()

    repeat(cols - 1, lambda step: wa_copy(step).wait_recv())
    w_row[me_r] = jnp.sum(w_col[...].astype(jnp.float32), axis=0).astype(WIRE)
    repeat(rows - 1, lambda turn: wb_copy(row_order(turn)).start())
    for part in range(parts):
        repeat(cols - 2, lambda turn: back_copy(part, col_first(turn + 1)).start())


    split_copy.wait_send()
    repeat(cols - 1, lambda step: gather_copy(step).wait_send())
    repeat(rows - 1, lambda step: part_copy(step).wait_send())
    for part in range(parts):
        repeat(rows - 1, lambda step: delta_copy(part, step).wait_send())

    grad = jnp.zeros((width, own), jnp.float32)
    for part in range(parts):
        if part == parts - 1:
            repeat(rows - 1, lambda step: wb_copy(step).wait_recv())
            for k in range(2):
                total = w_row[k].astype(jnp.float32)
                for pair in range(1, pairs):
                    total = total + w_row[2 * pair + k].astype(jnp.float32)
                weight_grad[k * half : (k + 1) * half] = total[:half] * norm
                if k == 0:
                    bias_grad[...] = total[half : half + 1] * norm

        repeat(cols - 1, lambda step: back_copy(part, step).wait_recv())
        back_sum = backs[part] + jnp.sum(back_recv[part].astype(jnp.float32), axis=0)
        grad = grad + dot(weight_out[part], stacked_right(degree[...] * back_sum))
    feature_grad[...] = grad.T

    for copy in (wa_copy,):
        repeat(cols - 1, lambda step, copy=copy: copy(step).wait_send())
    repeat(rows - 1, lambda step: wb_copy(step).wait_send())
    for part in range(parts):
        repeat(cols - 1, lambda step: back_copy(part, step).wait_send())


def write_out(*refs):
    *refs, sem = refs
    half = len(refs) // 2
    copies = [
        pltpu.make_async_copy(refs[index], refs[half + index], sem.at[index])
        for index in range(half)
    ]
    for copy in copies:
        copy.start()
    for copy in copies:
        copy.wait()


def local(
    features, weight, layer_bias, degree_scale, tile_values, tile_slots, tile_count, cotangent
):
    own, width = features.shape
    slots, tile = tile_values.shape[2:4]
    rows = lax.axis_size("row")
    cols = lax.axis_size("col")
    sub = own // tile
    places = rows * sub * cols * sub
    parts = 2
    chunk, half, pairs = width // parts, width // 2, rows // 2
    norm = 1.0 / math.sqrt(own * rows * cols)

    f32, bf16, i32 = jnp.float32, jnp.bfloat16, jnp.int32
    vmem = pl.BlockSpec(memory_space=pltpu.VMEM)
    r1, c1 = (rows - 1,), (cols - 1,)
    r2, c2 = (parts, rows - 1), (parts, cols - 1)
    dma = pltpu.SemaphoreType.DMA
    out_shape = (
        jax.ShapeDtypeStruct((own, width), f32),
        jax.ShapeDtypeStruct((own, width), f32),
        jax.ShapeDtypeStruct((width, width), f32),
        jax.ShapeDtypeStruct((1, width), f32),
    )
    outs = pl.pallas_call(
        functools.partial(kernel, rows, cols, norm),
        out_shape=tuple(pltpu.VMEM(out.shape, out.dtype) for out in out_shape),
        in_specs=[pl.BlockSpec(memory_space=pltpu.HBM)] * 8,
        out_specs=(vmem, vmem, vmem, vmem),
        scratch_shapes=[
            pltpu.VMEM((own, width), f32),
            pltpu.VMEM((width, width), f32),
            pltpu.VMEM((1, width), f32),
            pltpu.VMEM((1, own), f32),
            pltpu.VMEM((own, width), f32),
            pltpu.VMEM((1, slots), i32),
            pltpu.VMEM((1,), i32),
            pltpu.VMEM((places, 128), i32),
            pltpu.SMEM((places, 128), i32),
            pltpu.VMEM((slots + 1, tile, tile), bf16),
            pltpu.VMEM((pairs, 2 * own, cols * own), bf16),
            pltpu.VMEM((pairs, cols * own, 2 * own), bf16),
            pltpu.VMEM((cols, width, own), bf16),
            pltpu.VMEM((rows - 1, width, own), WIRE),
            pltpu.VMEM((rows - 1, width, own), WIRE),
            pltpu.VMEM((parts, rows, chunk, own), bf16),
            pltpu.VMEM((width, own), f32),
            pltpu.VMEM((width, own), f32),
            pltpu.VMEM((width, 3 * width), bf16),
            pltpu.VMEM((parts, width, 3 * chunk), bf16),
            pltpu.VMEM((parts, cols, chunk, own), WIRE),
            pltpu.VMEM((parts, cols - 1, chunk, own), WIRE),
            pltpu.VMEM((2, half + 8, width), f32),
            pltpu.VMEM((half + 8, width), f32),
            pltpu.VMEM((cols, half + 16, width), WIRE),
            pltpu.VMEM((rows, half + 16, width), WIRE),
            dma((7,)), dma, dma, dma(c1), dma(c1), dma(r1), dma(r1), dma(r2), dma(r2),
            dma(c2), dma(c2), dma(c1), dma(c1), dma(r1), dma(r1), dma, dma,
        ],
        compiler_params=pltpu.CompilerParams(collective_id=0, has_side_effects=True),
        name="graph_layer",
    )(
        features, weight, layer_bias.reshape(1, width), degree_scale.reshape(1, own),
        cotangent, tile_values.reshape(slots, tile, tile), tile_slots.reshape(1, slots),
        tile_count.reshape(1),
    )
    outs = pl.pallas_call(
        write_out,
        out_shape=out_shape,
        in_specs=[vmem] * 4,
        out_specs=[pl.BlockSpec(memory_space=pltpu.HBM)] * 4,
        scratch_shapes=[dma((4,))],
        name="write_out",
    )(*[pltpu.with_memory_space_constraint(out, pltpu.VMEM) for out in outs])
    return (outs[0], outs[1], outs[2], outs[3].reshape(width))


def solution(mesh):
    return jax.shard_map(
        local,
        mesh=mesh,
        in_specs=(
            P(("row", "col"), None),
            P(),
            P(),
            P(("row", "col")),
            P("row", "col", None, None, None),
            P("row", "col", None),
            P("row", "col"),
            P(("row", "col"), None),
        ),
        out_specs=(P(("row", "col"), None), P(("row", "col"), None), P(), P()),
        check_vma=False,
    )
```

```python
import functools
import math

import jax
import jax.numpy as jnp
from jax import lax
from jax.experimental import pallas as pl
from jax.experimental.pallas import tpu as pltpu
from jax.sharding import PartitionSpec as P

MESH = pl.DeviceIdType.MESH
WIRE = jnp.bfloat16


def gelu_pair(values):
    argument = 0.7978845608028654 * (values + 0.044715 * values * values * values)
    tangent = jnp.tanh(argument)
    output = 0.5 * values * (1.0 + tangent)
    slopes = 0.5 * (1.0 + tangent) + 0.5 * values * (
        1.0 - tangent * tangent
    ) * 0.7978845608028654 * (1.0 + 3.0 * 0.044715 * values * values)
    return (output, slopes)


def repeat(count, body):
    if count <= 8:
        for index in range(count):
            body(index)
    else:
        lax.fori_loop(0, count, lambda index, carry: (body(index), carry)[1], 0)


def dot(a, b, **kw):
    return jnp.dot(a, b, preferred_element_type=jnp.float32, **kw)


def halves(values):
    high = values.astype(jnp.bfloat16)
    return high, (values - high.astype(jnp.float32)).astype(jnp.bfloat16)


def stacked_left(matrix):
    high, low = halves(matrix)
    return jnp.concatenate([high, low, high], axis=1)


def stacked_right(values):
    high, low = halves(values)
    return jnp.concatenate([high, high, low], axis=0)


def dot_t(a, b):
    return lax.dot_general(a, b, (((1,), (1,)), ((), ())), preferred_element_type=jnp.float32)


def kernel(
    rows, cols, norm,
    features_hbm, weight_hbm, bias_hbm, degree_hbm, cotangent_hbm, tile_hbm, slot_hbm, count_hbm,
    activation, feature_grad, weight_grad, bias_grad,
    features, weight, bias, degree, cotangent, slot_list, live, found, inverse,
    tiles, dense, dense_t, gathered, part_send, part_recv, delta_all,
    bias_column, cotangent_turned, weight_in, weight_out,
    back_send, back_recv, w_part, w_core, w_col, w_row,
    in_sem, tile_sem, found_sem, g_send, g_recv, p_send, p_recv, d_send, d_recv,
    b_send, b_recv, wa_send, wa_recv, wb_send, wb_recv, wc_send, wc_recv,
):
    own, width = features.shape
    slots, tile, _ = tile_hbm.shape
    sub = own // tile
    places = found.shape[0]
    parts, _, chunk, _ = delta_all.shape
    pairs, half = rows // 2, width // 2
    me_r = lax.axis_index("row")
    me_c = lax.axis_index("col")
    me_p, me_k = lax.div(me_r, jnp.int32(2)), lax.rem(me_r, 2)

    def row_peer(step):
        return lax.rem(me_r + step + 1, rows)

    def col_peer(step):
        return lax.rem(me_c + step + 1, cols)

    def pair_at(turn):
        peer, bit = 0, 1
        while bit < pairs:
            flipped = lax.rem(lax.div(me_p, jnp.int32(bit)) + turn // bit, 2)
            peer, bit = peer + bit * flipped, bit * 2
        return peer

    def step_to(peer):
        return lax.rem(peer - me_r - 1 + rows, rows)

    def step_from(peer):
        return lax.rem(me_r - peer - 1 + rows, rows)

    def row_order(turn):
        other = rows - 1 - turn
        peer, bit = 0, 1
        while bit < rows:
            flipped = lax.rem(lax.div(me_r, jnp.int32(bit)) + other // bit, 2)
            peer, bit = peer + bit * flipped, bit * 2
        return step_to(peer)

    def col_order(turn):
        down = cols - 1 - turn
        down = down - lax.div(me_c - down + cols, cols)
        up = turn + lax.div(turn - me_c + cols, cols)
        high = lax.div(me_c * 2, cols)
        peer = high * up + (1 - high) * down
        return lax.rem(peer - me_c - 1 + cols, cols)

    def row_first(turn):
        return step_to(turn + lax.div(turn - me_r + rows, rows))

    def col_first(turn):
        peer = turn + lax.div(turn - me_c + cols, cols)
        return lax.rem(peer - me_c - 1 + cols, cols)

    def to_row(step, src, dst, send, recv):
        return pltpu.make_async_remote_copy(
            src_ref=src, dst_ref=dst, send_sem=send.at[step], recv_sem=recv.at[step],
            device_id=(row_peer(step), me_c), device_id_type=MESH,
        )

    def to_col(step, src, dst, send, recv):
        return pltpu.make_async_remote_copy(
            src_ref=src, dst_ref=dst, send_sem=send.at[step], recv_sem=recv.at[step],
            device_id=(me_r, col_peer(step)), device_id_type=MESH,
        )

    barrier = pltpu.get_barrier_semaphore()

    def greet_row(step):
        pl.semaphore_signal(barrier, inc=1, device_id=(row_peer(step), me_c), device_id_type=MESH)

    def greet_col(step):
        pl.semaphore_signal(barrier, inc=1, device_id=(me_r, col_peer(step)), device_id_type=MESH)

    repeat(cols - 1, greet_col)
    repeat(rows - 1, greet_row)
    loads = [
        pltpu.make_async_copy(src, dst, in_sem.at[index])
        for index, (src, dst) in enumerate((
            (features_hbm, features), (degree_hbm, degree), (slot_hbm, slot_list),
            (count_hbm, live), (weight_hbm, weight), (bias_hbm, bias), (cotangent_hbm, cotangent),
        ))
    ]
    for load in loads:
        load.start()
    tile_copy = pltpu.make_async_copy(tile_hbm, tiles.at[pl.ds(0, slots)], tile_sem)
    tile_copy.start()
    tiles[slots] = jnp.zeros((tile, tile), tiles.dtype)
    for load in loads[:4]:
        load.wait()

    scaled = (features[...].T * degree[...]).astype(jnp.bfloat16)
    gathered[me_c] = scaled

    pl.semaphore_wait(barrier, rows + cols - 2)

    def gather_copy(step):
        return to_col(step, gathered.at[me_c], gathered.at[me_c], g_send, g_recv)

    repeat(cols - 1, lambda turn: gather_copy(col_order(turn)).start())

    order = lax.broadcasted_iota(jnp.int32, (places, slots), 1)
    spot = lax.broadcasted_iota(jnp.int32, (places, slots), 0)
    hit = (slot_list[...] == spot) & (order < live[...][:, None])
    nearest = jnp.min(jnp.where(hit, order, slots), axis=1, keepdims=True)
    found[...] = jnp.broadcast_to(nearest, found.shape)
    found_copy = pltpu.make_async_copy(found, inverse, found_sem)
    found_copy.start()
    for load in loads[4:]:
        load.wait()
    turned = weight[...].T
    weight_in[...] = stacked_left(turned)
    for part in range(parts):
        weight_out[part] = stacked_left(weight[:, part * chunk : (part + 1) * chunk])
    bias_column[...] = jnp.broadcast_to(bias[...], (own, width)).T
    cotangent_turned[...] = cotangent[...].T
    found_copy.wait()
    tile_copy.wait()

    def place(pair):
        for u in range(2 * sub):
            for v in range(cols * sub):
                block = tiles[inverse[(pair * 2 * sub + u) * (cols * sub) + v, 0]]
                dense[pair, u * tile : (u + 1) * tile, v * tile : (v + 1) * tile] = block
                dense_t[pair, v * tile : (v + 1) * tile, u * tile : (u + 1) * tile] = block.T

    repeat(pairs, place)

    def part_copy(step):
        return to_row(step, part_send.at[step], part_recv.at[step], p_send, p_recv)

    repeat(cols - 1, lambda step: gather_copy(step).wait_recv())
    source = jnp.concatenate([gathered[v] for v in range(cols)], axis=1)

    def send_pair(turn):
        pair = pair_at(pairs - 1 - turn)
        result = dot(source, dense_t[pair])
        for k in range(2):
            step = step_to(pair * 2 + k)
            part_send[step] = result[:, k * own : (k + 1) * own].astype(WIRE)
            part_copy(step).start()

    repeat(pairs - 1, send_pair)
    result = dot(source, dense_t[me_p])
    first, second = result[:, :own], result[:, own:]
    core = step_to(me_p * 2 + 1 - me_k)
    part_send[core] = jnp.where(me_k == 0, second, first).astype(WIRE)
    part_copy(core).start()
    own_part = jnp.where(me_k == 0, first, second)

    repeat(rows - 1, lambda step: part_copy(step).wait_recv())
    aggregate = own_part + jnp.sum(part_recv[...].astype(jnp.float32), axis=0)
    stacked = stacked_right(aggregate)

    def delta_copy(part, step):
        mine = delta_all.at[part, me_r]
        return to_row(step, mine, mine, d_send.at[part], d_recv.at[part])

    outputs, deltas = [], []
    for part in range(parts):
        span = slice(part * chunk, (part + 1) * chunk)
        summed = dot(weight_in[span], stacked)
        output, slopes = gelu_pair(degree[...] * summed + bias_column[span])
        delta = cotangent_turned[span] * slopes
        delta_all[part, me_r] = (degree[...] * delta).astype(jnp.bfloat16)
        repeat(rows - 1, lambda turn: delta_copy(part, row_first(turn)).start())
        outputs.append(output)
        deltas.append(delta)
    output, delta = jnp.concatenate(outputs, axis=0), jnp.concatenate(deltas, axis=0)
    delta_scaled = jnp.concatenate([delta_all[part, me_r] for part in range(parts)], axis=0)

    high, low = halves(aggregate)
    terms = dot_t(high, delta_scaled) + dot_t(low, delta_scaled)
    bias_term = jnp.broadcast_to(jnp.sum(delta.T, axis=0, keepdims=True), (8, width))
    for k in range(2):
        w_part[k, :half] = terms[k * half : (k + 1) * half]
        w_part[k, half:] = bias_term

    def to_core(src, dst, send, recv):
        return pltpu.make_async_remote_copy(
            src_ref=src, dst_ref=dst, send_sem=send, recv_sem=recv,
            device_id=(me_p * 2 + 1 - me_k, me_c), device_id_type=MESH,
        )

    split_copy = to_core(w_part.at[1 - me_k], w_core, wc_send, wc_recv)
    split_copy.start()
    activation[...] = output.T
    split_copy.wait_recv()

    def packed(values):
        values = values.astype(WIRE)
        return values[:half], jnp.broadcast_to(values[half : half + 1], (16, width))

    w_col[me_c, :half], w_col[me_c, half:] = packed(w_part[me_k] + w_core[...])

    def wa_copy(step):
        return to_col(step, w_col.at[me_c], w_col.at[me_c], wa_send, wa_recv)

    repeat(cols - 1, lambda turn: wa_copy(col_order(turn)).start())

    def wb_copy(step):
        return to_row(step, w_row.at[me_r], w_row.at[me_r], wb_send, wb_recv)

    def back_copy(part, step):
        return to_col(
            step, back_send.at[part, col_peer(step)], back_recv.at[part, step], b_send.at[part], b_recv.at[part]
        )

    def arrived(part, turn):
        pair = pair_at(turn)
        for k in range(2):
            delta_copy(part, step_from(pair * 2 + k)).wait_recv()

    def back_term(part, pair):
        left = jnp.concatenate([delta_all[part, pair * 2 + k] for k in range(2)], axis=1)
        return dot(left, dense[pair])

    backs = []
    for part in range(parts):
        delta_copy(part, step_from(me_p * 2 + 1 - me_k)).wait_recv()
        total = back_term(part, me_p)

        def add_pair(turn, total):
            arrived(part, turn)
            return total + back_term(part, pair_at(turn))

        if pairs <= 8:
            for turn in range(1, pairs):
                total = add_pair(turn, total)
        else:
            total = lax.fori_loop(1, pairs, add_pair, total)

        mine = jnp.zeros((chunk, own), jnp.float32)
        for v in range(cols):
            block = total[:, v * own : (v + 1) * own]
            mine = jnp.where(me_c == v, block, mine)
            back_send[part, v] = block.astype(WIRE)
        backs.append(mine)
        if part < parts - 1:
            back_copy(part, col_first(0)).start()
        else:

            @pl.when(me_k == 0)
            def _():
                back_copy(part, col_first(0)).start()


    repeat(cols - 1, lambda step: wa_copy(step).wait_recv())
    w_row[me_r] = jnp.sum(w_col[...].astype(jnp.float32), axis=0).astype(WIRE)

    @pl.when(me_k == 1)
    def _():
        back_copy(parts - 1, col_first(0)).start()

    repeat(rows - 1, lambda turn: wb_copy(row_order(turn)).start())
    for part in range(parts):
        repeat(cols - 2, lambda turn: back_copy(part, col_first(turn + 1)).start())


    grad = jnp.zeros((width, own), jnp.float32)
    for part in range(parts):
        if part == parts - 1:
            repeat(rows - 1, lambda step: wb_copy(step).wait_recv())
            for k in range(2):
                total = w_row[k].astype(jnp.float32)
                for pair in range(1, pairs):
                    total = total + w_row[2 * pair + k].astype(jnp.float32)
                weight_grad[k * half : (k + 1) * half] = total[:half] * norm
                if k == 0:
                    bias_grad[...] = total[half : half + 1] * norm

        repeat(cols - 1, lambda step: back_copy(part, step).wait_recv())
        back_sum = backs[part] + jnp.sum(back_recv[part].astype(jnp.float32), axis=0)
        grad = grad + dot(weight_out[part], stacked_right(degree[...] * back_sum))
    feature_grad[...] = grad.T

    split_copy.wait_send()
    repeat(rows - 1, lambda step: wb_copy(step).wait_send())
    for copy in (gather_copy, wa_copy):
        repeat(cols - 1, lambda step, copy=copy: copy(step).wait_send())
    repeat(rows - 1, lambda step: part_copy(step).wait_send())
    for part in range(parts):
        repeat(cols - 1, lambda step: back_copy(part, step).wait_send())
        repeat(rows - 1, lambda step: delta_copy(part, step).wait_send())


def write_out(*refs):
    *refs, sem = refs
    half = len(refs) // 2
    copies = [
        pltpu.make_async_copy(refs[index], refs[half + index], sem.at[index])
        for index in range(half)
    ]
    for copy in copies:
        copy.start()
    for copy in copies:
        copy.wait()


def local(
    features, weight, layer_bias, degree_scale, tile_values, tile_slots, tile_count, cotangent
):
    own, width = features.shape
    slots, tile = tile_values.shape[2:4]
    rows = lax.axis_size("row")
    cols = lax.axis_size("col")
    sub = own // tile
    places = rows * sub * cols * sub
    parts = 2
    chunk, half, pairs = width // parts, width // 2, rows // 2
    norm = 1.0 / math.sqrt(own * rows * cols)

    f32, bf16, i32 = jnp.float32, jnp.bfloat16, jnp.int32
    vmem = pl.BlockSpec(memory_space=pltpu.VMEM)
    r1, c1 = (rows - 1,), (cols - 1,)
    r2, c2 = (parts, rows - 1), (parts, cols - 1)
    dma = pltpu.SemaphoreType.DMA
    out_shape = (
        jax.ShapeDtypeStruct((own, width), f32),
        jax.ShapeDtypeStruct((own, width), f32),
        jax.ShapeDtypeStruct((width, width), f32),
        jax.ShapeDtypeStruct((1, width), f32),
    )
    outs = pl.pallas_call(
        functools.partial(kernel, rows, cols, norm),
        out_shape=tuple(pltpu.VMEM(out.shape, out.dtype) for out in out_shape),
        in_specs=[pl.BlockSpec(memory_space=pltpu.HBM)] * 8,
        out_specs=(vmem, vmem, vmem, vmem),
        scratch_shapes=[
            pltpu.VMEM((own, width), f32),
            pltpu.VMEM((width, width), f32),
            pltpu.VMEM((1, width), f32),
            pltpu.VMEM((1, own), f32),
            pltpu.VMEM((own, width), f32),
            pltpu.VMEM((1, slots), i32),
            pltpu.VMEM((1,), i32),
            pltpu.VMEM((places, 128), i32),
            pltpu.SMEM((places, 128), i32),
            pltpu.VMEM((slots + 1, tile, tile), bf16),
            pltpu.VMEM((pairs, 2 * own, cols * own), bf16),
            pltpu.VMEM((pairs, cols * own, 2 * own), bf16),
            pltpu.VMEM((cols, width, own), bf16),
            pltpu.VMEM((rows - 1, width, own), WIRE),
            pltpu.VMEM((rows - 1, width, own), WIRE),
            pltpu.VMEM((parts, rows, chunk, own), bf16),
            pltpu.VMEM((width, own), f32),
            pltpu.VMEM((width, own), f32),
            pltpu.VMEM((width, 3 * width), bf16),
            pltpu.VMEM((parts, width, 3 * chunk), bf16),
            pltpu.VMEM((parts, cols, chunk, own), WIRE),
            pltpu.VMEM((parts, cols - 1, chunk, own), WIRE),
            pltpu.VMEM((2, half + 8, width), f32),
            pltpu.VMEM((half + 8, width), f32),
            pltpu.VMEM((cols, half + 16, width), WIRE),
            pltpu.VMEM((rows, half + 16, width), WIRE),
            dma((7,)), dma, dma, dma(c1), dma(c1), dma(r1), dma(r1), dma(r2), dma(r2),
            dma(c2), dma(c2), dma(c1), dma(c1), dma(r1), dma(r1), dma, dma,
        ],
        compiler_params=pltpu.CompilerParams(collective_id=0, has_side_effects=True),
        name="graph_layer",
    )(
        features, weight, layer_bias.reshape(1, width), degree_scale.reshape(1, own),
        cotangent, tile_values.reshape(slots, tile, tile), tile_slots.reshape(1, slots),
        tile_count.reshape(1),
    )
    outs = pl.pallas_call(
        write_out,
        out_shape=out_shape,
        in_specs=[vmem] * 4,
        out_specs=[pl.BlockSpec(memory_space=pltpu.HBM)] * 4,
        scratch_shapes=[dma((4,))],
        name="write_out",
    )(*[pltpu.with_memory_space_constraint(out, pltpu.VMEM) for out in outs])
    return (outs[0], outs[1], outs[2], outs[3].reshape(width))


def solution(mesh):
    return jax.shard_map(
        local,
        mesh=mesh,
        in_specs=(
            P(("row", "col"), None),
            P(),
            P(),
            P(("row", "col")),
            P("row", "col", None, None, None),
            P("row", "col", None),
            P("row", "col"),
            P(("row", "col"), None),
        ),
        out_specs=(P(("row", "col"), None), P(("row", "col"), None), P(), P()),
        check_vma=False,
    )
```
